32 devices in a mesh: dp: 4 (over y, x), shard: 8 (over z, core).
Axes of the slice: x: 2, y: 2, z: 4, core: 2. Of those that a mesh axis runs over, the one named last changes fastest.
Arguments:
- id_table: float32 [262144, 128], P(('dp', 'shard')), may hold values from -6 to 6
- ada_state: float32 [262144], P(('dp', 'shard')), may hold values from 0.01 to 1
- user_first: float32 [128, 512], replicated, may hold values from -0.5 to 0.5
- user_second: float32 [512, 128], replicated, may hold values from -0.25 to 0.25
- item_first: float32 [128, 512], replicated, may hold values from -0.5 to 0.5
- item_second: float32 [512, 128], replicated, may hold values from -0.25 to 0.25
- fetch_rows: int32 [32, 4, 8, 72], P(('dp', 'shard')), may hold values from 0 to 8191
- lookup_slots: int32 [32, 1536], P(('dp', 'shard')), may hold values from 0 to 2303
Outputs:
- new_table: float32 [262144, 128], P(('dp', 'shard'))
- new_state: float32 [262144], P(('dp', 'shard'))
- user_first_grad: float32 [128, 512], replicated
- user_second_grad: float32 [512, 128], replicated
- item_first_grad: float32 [128, 512], replicated
- item_second_grad: float32 [512, 128], replicated
- mean_loss: float32 [], replicated
The draws below stay inside these ranges and needn't reach their ends.
All inputs are finite; a program needn't handle non-finite values.
Results may differ from the reference program's by a relative error of at most 0.0038.
The reference program's roundings to bfloat16 on the way count: a program that leaves them out, or rounds other values in their place, can miss the bound.
Values may be sent and summed in bfloat16 or wider, within the bound.
No kernel may reach another device: no remote copies, remote signals or barrier semaphores. Data moves between devices by JAX's collectives and lax.ppermute only.
A program may use at most 128 MiB of HBM per device.

```python
import math
import jax
import jax.numpy as jnp
import numpy as np
from jax import lax

D = 128
HIDDEN_SIZE = 512
ROWS_DEV = 8192
EXAMPLES_ON_CHIP = 512
LOOK_DEV = 1536
CAND_DEV = 1024
CAP = 72
TABLE_ROWS = 262144
N_DP = 4
N_SHARD = 8


def with_ends(entries, rng, low, top_value):
    longest = entries.shape.index(max(entries.shape))
    spots = []
    for shift in (0, 1):
        where = [jax.random.randint(jax.random.fold_in(rng, axis), (), 0, length) for axis, length in enumerate(entries.shape)]
        where[longest] = (where[longest] + shift) % entries.shape[longest]
        spots.append(tuple(where))
    return entries.at[spots[0]].set(low).at[spots[1]].set(top_value)


def steps_of(key, extent, split, low, top_value):
    level, own = 1.0, jax.random.fold_in(key, 6)
    for position, blocks in split:
        draws = jnp.exp(jax.random.uniform(jax.random.fold_in(own, position), (blocks,), jnp.float32, low / len(split), top_value / len(split)))
        level = level * jnp.repeat(draws, extent[position] // blocks).reshape([-1 if axis == position else 1 for axis in range(len(extent))])
    return level


def rank_table(number_of, skew):
    weights = [(1 << 20) // math.isqrt(grade ** skew) + 1 for grade in range(1, number_of + 1)]
    scale = 1 + sum(weights) // (1 << 30)
    return np.cumsum(np.array([max(1, weight // scale) for weight in weights]))


def skewed_ids(own_key, shape, count, lean):
    listing = rank_table(count, lean)
    ticket = jax.random.randint(jax.random.fold_in(own_key, 1), shape, 0, int(listing[count - 1]))
    grade = jnp.searchsorted(jnp.asarray(listing, jnp.int32), ticket, side="right")
    return jax.random.permutation(jax.random.fold_in(own_key, 2), count)[grade].astype(jnp.int32)


def bell_draw(key, dims, deviation, limit, cuts=(), held_as=jnp.bfloat16):
    entries = deviation * jax.random.normal(key, dims, jnp.float32)
    if cuts:
        entries = entries * steps_of(key, dims, cuts, -0.22, 0.18)
    return jnp.clip(entries, -limit, limit).astype(held_as)


def setup_inputs(seed: int = 0) -> dict:
    seeds = jax.random.split(jax.random.key(seed), 9)
    id_table = bell_draw(seeds[0], (TABLE_ROWS, D), 1.0, 6.0, ((0, 32),), jnp.float32)
    ada_state = jnp.clip(jnp.exp(math.log(1.0) - 4.6051702 * jax.random.uniform(seeds[1], (TABLE_ROWS,), jnp.float32) ** steps_of(seeds[1], (TABLE_ROWS,), ((0, 32),), -0.2, 0.2)), 0.01, 1.0)
    user_first = bell_draw(seeds[2], (D, HIDDEN_SIZE), D ** -0.5, 0.5, (), jnp.float32)
    user_second = bell_draw(seeds[3], (HIDDEN_SIZE, D), HIDDEN_SIZE ** -0.5, 0.25, (), jnp.float32)
    item_first = bell_draw(seeds[4], (D, HIDDEN_SIZE), D ** -0.5, 0.5, (), jnp.float32)
    item_second = bell_draw(seeds[5], (HIDDEN_SIZE, D), HIDDEN_SIZE ** -0.5, 0.25, (), jnp.float32)
    fetch_rows = with_ends(jax.random.randint(seeds[6], (N_DP * N_SHARD, N_DP, N_SHARD, CAP), 0, ROWS_DEV), jax.random.fold_in(seeds[6], 1), 0, ROWS_DEV - 1).astype(jnp.int32)
    lookup_slots = with_ends(skewed_ids(seeds[7], (N_DP * N_SHARD, LOOK_DEV), N_DP * N_SHARD * CAP, 1), jax.random.fold_in(seeds[7], 3), 0, (N_DP * N_SHARD * CAP) - 1).astype(jnp.int32)
    return {"id_table": id_table, "ada_state": ada_state, "user_first": user_first, "user_second": user_second, "item_first": item_first, "item_second": item_second, "fetch_rows": fetch_rows, "lookup_slots": lookup_slots}


highest = lax.Precision.HIGHEST
logit_divisor = 0.025
learn_rate = 0.1
epsilon = 1e-08

def tower_pass(looked, first_w, second_w):
    hidden_act = jax.nn.silu(jnp.dot(looked, first_w, precision=highest, preferred_element_type=jnp.float32))
    tower_out = jnp.dot(hidden_act, second_w, precision=highest, preferred_element_type=jnp.float32)
    return tower_out / jnp.sqrt(lax.optimization_barrier(jnp.sum(tower_out * tower_out, axis=1, keepdims=True)) + 1e-06)

def one_group(pair):
    pooled_queries, pooled_targets = pair
    logit_table = jnp.dot(pooled_queries, pooled_targets.T, preferred_element_type=jnp.float32) / logit_divisor
    exponent = jnp.exp(logit_table)
    reduced_aggregates = lax.optimization_barrier(jnp.sum(exponent, axis=1))
    collected_entries = jnp.dot(exponent.astype(jnp.bfloat16), pooled_targets, preferred_element_type=jnp.float32)
    log_z = jnp.log(reduced_aggregates)
    softmax = jnp.exp(logit_table - log_z[:, None]).astype(jnp.bfloat16)
    target_derivative_accrual = jnp.dot(softmax.T, pooled_queries, preferred_element_type=jnp.float32)
    return (reduced_aggregates, collected_entries, log_z, target_derivative_accrual)

def reference(id_table, ada_state, user_first, user_second, item_first, item_second, fetch_rows, lookup_slots):
    shard_number = N_DP * N_SHARD
    target_index_vector = id_table.shape[1]
    owners = jnp.arange(shard_number * CAP, dtype=jnp.int32) // CAP * ROWS_DEV
    row_map = fetch_rows.reshape(shard_number, shard_number * CAP) + owners[None, :]
    row_ids = jnp.take_along_axis(row_map, lookup_slots, axis=1)
    looked = jnp.take(id_table, row_ids.reshape(-1), axis=0).reshape(shard_number, LOOK_DEV, target_index_vector)
    user_in = looked[:, :EXAMPLES_ON_CHIP].reshape(-1, target_index_vector)
    item_in = looked[:, EXAMPLES_ON_CHIP:].reshape(-1, target_index_vector)
    user_vec, user_pull = jax.vjp(tower_pass, user_in, user_first, user_second)
    item_vec, item_pull = jax.vjp(tower_pass, item_in, item_first, item_second)
    user_half_precision = user_vec.astype(jnp.bfloat16)
    item_bf = item_vec.astype(jnp.bfloat16)
    pooled_queries = user_half_precision.reshape(N_DP, N_SHARD, EXAMPLES_ON_CHIP, target_index_vector).transpose(1, 0, 2, 3).reshape(N_SHARD, N_DP * EXAMPLES_ON_CHIP, target_index_vector)
    pooled_targets = item_bf.reshape(N_DP, N_SHARD, CAND_DEV, target_index_vector).transpose(1, 0, 2, 3).reshape(N_SHARD, N_DP * CAND_DEV, target_index_vector)
    reduced_aggregates, collected_entries, log_z, target_derivative_accrual = lax.map(one_group, (pooled_queries, pooled_targets))
    reduced_aggregates = reduced_aggregates.reshape(N_SHARD, N_DP, EXAMPLES_ON_CHIP).transpose(1, 0, 2).reshape(-1)
    log_z = log_z.reshape(N_SHARD, N_DP, EXAMPLES_ON_CHIP).transpose(1, 0, 2).reshape(-1)
    collected_entries = collected_entries.reshape(N_SHARD, N_DP, EXAMPLES_ON_CHIP, target_index_vector).transpose(1, 0, 2, 3).reshape(-1, target_index_vector)
    target_derivative_accrual = target_derivative_accrual.reshape(N_SHARD, N_DP, CAND_DEV, target_index_vector).transpose(1, 0, 2, 3).reshape(shard_number, CAND_DEV, target_index_vector)
    resident_target_entries = item_bf.reshape(shard_number, CAND_DEV, target_index_vector)[:, :EXAMPLES_ON_CHIP].reshape(-1, target_index_vector).astype(jnp.float32)
    query_single_float = user_half_precision.astype(jnp.float32)
    matching_pair_logit = lax.optimization_barrier(jnp.sum(query_single_float * resident_target_entries, axis=1)) / logit_divisor
    query_adjoint = (collected_entries / reduced_aggregates[:, None] - resident_target_entries) / logit_divisor
    target_adjoint = target_derivative_accrual.at[:, :EXAMPLES_ON_CHIP].add(-query_single_float.reshape(shard_number, EXAMPLES_ON_CHIP, target_index_vector)).reshape(-1, target_index_vector) / logit_divisor
    user_look, user_first_g, user_second_g = user_pull(query_adjoint)
    item_look, item_first_g, item_second_g = item_pull(target_adjoint)
    look_grads = jnp.concatenate([user_look.reshape(shard_number, EXAMPLES_ON_CHIP, target_index_vector), item_look.reshape(shard_number, CAND_DEV, target_index_vector)], axis=1).reshape(-1, target_index_vector)
    grad_rows = jnp.zeros_like(id_table).at[row_ids.reshape(-1)].add(look_grads)
    new_state = ada_state + lax.optimization_barrier(jnp.mean(grad_rows * grad_rows, axis=1))
    new_table = id_table - learn_rate * grad_rows / (jnp.sqrt(new_state)[:, None] + epsilon)
    mean_loss = jnp.sum(log_z - matching_pair_logit) / (shard_number * EXAMPLES_ON_CHIP)
    return (new_table, new_state, user_first_g / shard_number, user_second_g / shard_number, item_first_g / shard_number, item_second_g / shard_number, mean_loss)
```

```python
import jax
import jax.numpy as jnp
from jax import lax
from jax.sharding import PartitionSpec as P

EXAMPLES_ON_CHIP = 512
AXES = ("dp", "shard")

highest = lax.Precision.HIGHEST
logit_divisor = 0.025
learn_rate = 0.1
epsilon = 1e-08


def tower_pass(looked, first_w, second_w):
    hidden_act = jax.nn.silu(
        jnp.dot(looked, first_w, precision=highest, preferred_element_type=jnp.float32)
    )
    tower_out = jnp.dot(hidden_act, second_w, precision=highest, preferred_element_type=jnp.float32)
    return tower_out / jnp.sqrt(jnp.sum(tower_out * tower_out, axis=1, keepdims=True) + 1e-06)


def exchange(x):
    return lax.all_to_all(x, AXES, split_axis=0, concat_axis=0, tiled=True)


def from_peers(blocks, n):
    out = [blocks[0]]
    for k in range(1, n):
        out.append(lax.ppermute(blocks[k], "dp", [(i, (i + k) % n) for i in range(n)]))
    return out


def to_owners(blocks, n):
    out = [blocks[0]]
    for k in range(1, n):
        out.append(lax.ppermute(blocks[k], "dp", [(i, (i - k) % n) for i in range(n)]))
    return out


def per_device(
    id_table, ada_state, user_first, user_second, item_first, item_second, fetch_rows, lookup_slots
):
    width = id_table.shape[1]
    n_dp = lax.axis_size("dp")
    n_all = n_dp * lax.axis_size("shard")
    cap = fetch_rows.shape[-1]
    n_ex = EXAMPLES_ON_CHIP
    asked = exchange(fetch_rows.reshape(n_all, cap))
    fetched = id_table.at[asked.reshape(-1)].get(mode="promise_in_bounds")
    slot_rows = exchange(fetched.reshape(n_all, cap, width)).reshape(-1, width)
    slot_index = lookup_slots[0]
    looked = slot_rows.at[slot_index].get(mode="promise_in_bounds")

    user_vec, user_pull = jax.vjp(tower_pass, looked[:n_ex], user_first, user_second)
    user_bf = user_vec.astype(jnp.bfloat16)
    group_users = from_peers([user_bf] * n_dp, n_dp)
    item_vec, item_pull = jax.vjp(tower_pass, looked[n_ex:], item_first, item_second)
    item_bf = item_vec.astype(jnp.bfloat16)

    parts, pulls, expos = [], [], []
    for block in group_users:
        expo = jnp.exp(
            jnp.dot(block, item_bf.T, preferred_element_type=jnp.float32) / logit_divisor
        )
        parts.append(jnp.sum(expo, axis=1))
        pulls.append(
            jnp.dot(expo.astype(jnp.bfloat16), item_bf, preferred_element_type=jnp.float32)
        )
        expos.append(expo)
    mine = jnp.stack(parts)
    seen = from_peers([mine] * n_dp, n_dp)
    totals = [sum(seen[k][(b - k) % n_dp] for k in range(n_dp)) for b in range(n_dp)]
    returned = to_owners([pulls[0]] + [p.astype(jnp.bfloat16) for p in pulls[1:]], n_dp)

    item_sum = sum(
        jnp.dot(
            (expo / total[:, None]).astype(jnp.bfloat16).T,
            block,
            preferred_element_type=jnp.float32,
        )
        for expo, total, block in zip(expos, totals, group_users)
    )
    user_f = user_bf.astype(jnp.float32)
    positive = item_bf[:n_ex].astype(jnp.float32)
    item_cot = (
        jnp.concatenate([item_sum[:n_ex] - user_f, item_sum[n_ex:]], axis=0) / logit_divisor
    )
    item_look, item_first_g, item_second_g = item_pull(item_cot)
    pulled = sum(p.astype(jnp.float32) for p in returned)
    user_cot = (pulled / totals[0][:, None] - positive) / logit_divisor
    user_look, user_first_g, user_second_g = user_pull(user_cot)
    pos_score = jnp.sum(user_f * positive, axis=1) / logit_divisor
    loss_part = jnp.sum(jnp.log(totals[0]) - pos_score)

    look_grads = jnp.concatenate([user_look, item_look], axis=0)
    slot_grads = jnp.zeros_like(slot_rows).at[slot_index].add(look_grads, mode="promise_in_bounds")
    weight_g = jnp.concatenate(
        [g.reshape(n_all, -1, width) for g in (user_first_g, user_second_g, item_first_g, item_second_g)],
        axis=1,
    )
    terms, rest = [], loss_part
    for _ in range(3):
        terms.append(lax.reduce_precision(rest, 8, 7))
        rest = rest - terms[-1]
    loss_row = jnp.concatenate([jnp.stack(terms), jnp.zeros(width - 3, jnp.float32)])
    sent = exchange(
        jnp.concatenate(
            [
                slot_grads.reshape(n_all, cap, width),
                weight_g,
                jnp.broadcast_to(loss_row, (n_all, 1, width)),
            ],
            axis=1,
        ).astype(jnp.bfloat16)
    )
    chunk = jnp.sum(sent[:, cap:-1].astype(jnp.float32), axis=0) / n_all
    whole = exchange(jnp.broadcast_to(chunk.astype(jnp.bfloat16)[None], weight_g.shape))
    mean_loss = jnp.sum(sent[:, -1, :3].astype(jnp.float32)) / (n_all * n_ex)

    grad_rows = (
        jnp.zeros_like(id_table)
        .at[asked.reshape(-1)]
        .add(sent[:, :cap].astype(jnp.float32).reshape(-1, width), mode="promise_in_bounds")
    )
    new_state = ada_state + jnp.mean(grad_rows * grad_rows, axis=1)
    new_table = id_table - learn_rate * grad_rows / (jnp.sqrt(new_state)[:, None] + epsilon)
    outs = []
    at = 0
    for w in (user_first, user_second, item_first, item_second):
        rows = w.size // (n_all * width)
        outs.append(whole[:, at : at + rows].astype(jnp.float32).reshape(w.shape))
        at += rows
    return (new_table, new_state, *outs, mean_loss)


def solution(mesh):
    return jax.shard_map(
        per_device,
        mesh=mesh,
        in_specs=(
            P(("dp", "shard"), None),
            P(("dp", "shard")),
            P(),
            P(),
            P(),
            P(),
            P(("dp", "shard"), None, None, None),
            P(("dp", "shard"), None),
        ),
        out_specs=(P(("dp", "shard"), None), P(("dp", "shard")), P(), P(), P(), P(), P()),
        check_vma=False,
    )
```

```python
import functools

import jax
import jax.numpy as jnp
from jax import lax
from jax.experimental import pallas as pl
from jax.experimental.pallas import tpu as pltpu
from jax.sharding import PartitionSpec as P

EXAMPLES_ON_CHIP = 512
AXES = ("dp", "shard")

fine = lax.Precision.HIGH
logit_divisor = 0.025
learn_rate = 0.1
epsilon = 1e-08


def product(a, b, dims):
    return lax.dot_general(
        a, b, (dims, ((), ())), precision=fine, preferred_element_type=jnp.float32
    )


def tower(looked, first_w, second_w):
    hidden = product(looked, first_w, ((1,), (0,)))
    gate = jax.nn.sigmoid(hidden)
    active = hidden * gate
    out = product(active, second_w, ((1,), (0,)))
    norm = jnp.sqrt(jnp.sum(out * out, axis=1, keepdims=True) + 1e-06)
    return out / norm, (looked, hidden, out, first_w, second_w)


def halves(x):
    high = x.astype(jnp.bfloat16)
    return high, (x - high.astype(jnp.float32)).astype(jnp.bfloat16)


def wide_dot(a, b, dims):
    def one(p, q):
        return lax.dot_general(p, q, (dims, ((), ())), preferred_element_type=jnp.float32)

    (ah, al), (bh, bl) = a, b
    return one(ah, bh) + one(al, bh) + one(ah, bl)


def back_kernel(last, *refs):
    looked, hidden, out, cot, first_w, second_w = refs[:6]
    first_g, second_g = refs[-2:]
    look_g = refs[-3] if last else refs[6]
    step = pl.program_id(0)

    @pl.when(step == 0)
    def _():
        first_g[...] = jnp.zeros_like(first_g)
        second_g[...] = jnp.zeros_like(second_g)

    z, g, h = out[...], cot[...], hidden[...]
    rows, width = z.shape
    inverse = 1.0 / jnp.sqrt(jnp.sum(z * z, axis=1, keepdims=True) + 1e-06)
    vec = z * inverse
    out_cot = (g - vec * jnp.sum(vec * g, axis=1, keepdims=True)) * inverse
    gate = 1.0 / (1.0 + jnp.exp(-h))
    active = h * gate
    slope = gate + active * (1.0 - gate)
    hidden_cot = wide_dot(halves(out_cot), halves(second_w[...]), ((1,), (1,))) * slope
    both = halves(hidden_cot)
    mine = wide_dot(both, halves(first_w[...]), ((1,), (1,))).astype(look_g.dtype)
    if last:
        look_g[pl.ds(pl.multiple_of(step * rows, rows), rows), :] = mine
    else:
        look_g[...] = mine
    first_g[...] += wide_dot(halves(looked[...].T), both, ((1,), (0,)))
    second_g[...] += wide_dot(halves(out_cot.T), halves(active), ((1,), (0,)))

    @pl.when(step == pl.num_programs(0) - 1)
    def _():
        flat = [first_g[:, c : c + width] for c in range(0, first_g.shape[1], width)]
        flat += [second_g[:, c : c + width].T for c in range(0, second_g.shape[1], width)]
        flat = [f.astype(jnp.bfloat16) for f in flat]
        if not last:
            for k, f in enumerate(flat):
                refs[7][k * width : (k + 1) * width, :] = f
            return
        item_look, item_sums, lookups, loss_row, sent = refs[6:11]
        n_all = sent.shape[0]
        deep = 2 * len(flat) * width // n_all
        cap = sent.shape[1] - deep - 8
        for k in range(n_all):
            block, at = divmod(k * deep, width)
            if block < len(flat):
                piece = flat[block][at : at + deep]
            else:
                at += (block - len(flat)) * width
                piece = item_sums[at : at + deep, :]
            sent[k, :deep, :] = piece
            sent[k, deep : deep + 8, :] = jnp.broadcast_to(loss_row[...], (8, width)).astype(
                sent.dtype
            )
        n_ex = look_g.shape[0]
        group = max(1, 576 // cap)
        user_ids, item_ids = lookups[:, :n_ex], lookups[:, n_ex:]
        for k in range(0, n_all, group):
            n = min(group, n_all - k)

            def owns(ids):
                slot = lax.broadcasted_iota(jnp.int32, (n * cap, ids.shape[1]), 0) + k * cap
                return jnp.where(slot == ids, 1.0, 0.0).astype(jnp.bfloat16)

            total = jnp.dot(owns(user_ids), look_g[...], preferred_element_type=jnp.float32)
            total += jnp.dot(owns(item_ids), item_look[...], preferred_element_type=jnp.float32)
            for j in range(n):
                sent[k + j, deep + 8 :, :] = total[j * cap : (j + 1) * cap].astype(sent.dtype)


def tower_back(saved, cot, rest=(), n_all=0, cap=0):
    looked, hidden, out, first_w, second_w = saved
    n, width = looked.shape
    inner = hidden.shape[1]
    rows = min(n, 256)
    last = bool(rest)

    def by_rows(w):
        return pl.BlockSpec((rows, w), lambda i: (i, 0))

    def fixed(shape):
        return pl.BlockSpec(shape, lambda i: (0,) * len(shape))

    if last:
        shape = (n_all, 4 * inner // n_all + 8 + cap, width)
        out_specs = fixed(shape)
        out_shape = jax.ShapeDtypeStruct(shape, jnp.bfloat16)
        scratch = [pltpu.VMEM((n, width), jnp.bfloat16)]
    else:
        out_specs = [by_rows(width), fixed((2 * inner, width))]
        out_shape = [
            jax.ShapeDtypeStruct((n, width), jnp.bfloat16),
            jax.ShapeDtypeStruct((2 * inner, width), jnp.bfloat16),
        ]
        scratch = []
    return pl.pallas_call(
        functools.partial(back_kernel, last),
        grid=(n // rows,),
        in_specs=[by_rows(width), by_rows(inner), by_rows(width), by_rows(width)]
        + [fixed(x.shape) for x in (first_w, second_w, *rest)],
        out_specs=out_specs,
        out_shape=out_shape,
        scratch_shapes=scratch + [pltpu.VMEM((width, inner), jnp.float32)] * 2,
        cost_estimate=pl.CostEstimate(
            flops=24 * n * width * inner,
            transcendentals=n * inner,
            bytes_accessed=4 * n * (inner + 4 * width),
        ),
        name="user_back" if last else "item_back",
    )(looked, hidden, out, cot, first_w, second_w, *rest)


def update_kernel(skip, rows_ref, grads, table, state, new_table, new_state, *totals):
    step = pl.program_id(0)

    @pl.when(step == 0)
    def _():
        for total in totals:
            total[...] = jnp.zeros_like(total)
        n_from, _, cap = rows_ref.shape
        each = n_from // len(totals)

        def body(i, carry):
            come = [grads[q * each + i, skip:, :].astype(jnp.float32) for q in range(len(totals))]
            for c in range(cap):
                for q, total in enumerate(totals):
                    row = rows_ref[q * each + i, 0, c]
                    total[pl.ds(row, 1), :] += come[q][c : c + 1, :]
            return carry

        lax.fori_loop(0, each, body, 0)

    rows, width = table.shape
    for k in range(rows // width):
        here = pl.ds(pl.multiple_of(step * rows + k * width, width), width)
        g = totals[0][here, :]
        for total in totals[1:]:
            g = g + total[here, :]
        mean = jnp.sum((g * g).T, axis=0, keepdims=True) * (1.0 / width)
        now = state[k : k + 1, :] + mean
        new_state[k : k + 1, :] = now
        scale = learn_rate / (jnp.sqrt(now) + epsilon)
        scale = jnp.broadcast_to(scale, (width, width)).T
        block = slice(k * width, (k + 1) * width)
        new_table[block, :] = table[block, :] - g * scale


def update(table, state, rows_of, grads):
    n, width = table.shape
    rows = n // 2
    lanes = 4
    state = state.reshape(-1, width)
    skip = grads.shape[1] - rows_of.shape[2]
    new_table, new_state = pl.pallas_call(
        functools.partial(update_kernel, skip),
        grid_spec=pltpu.PrefetchScalarGridSpec(
            num_scalar_prefetch=1,
            grid=(n // rows,),
            in_specs=[
                pl.BlockSpec(grads.shape, lambda i, r: (0, 0, 0)),
                pl.BlockSpec((rows, width), lambda i, r: (i, 0)),
                pl.BlockSpec((rows // width, width), lambda i, r: (i, 0)),
            ],
            out_specs=[
                pl.BlockSpec((rows, width), lambda i, r: (i, 0)),
                pl.BlockSpec((rows // width, width), lambda i, r: (i, 0)),
            ],
            scratch_shapes=[pltpu.VMEM(table.shape, jnp.float32)] * lanes,
        ),
        out_shape=[
            jax.ShapeDtypeStruct(table.shape, jnp.float32),
            jax.ShapeDtypeStruct(state.shape, jnp.float32),
        ],
        cost_estimate=pl.CostEstimate(
            flops=20 * n * width, transcendentals=n, bytes_accessed=8 * n * width
        ),
        name="update",
    )(rows_of, grads, table, state)
    return new_table, new_state.reshape(-1)


def spread_kernel(place, *refs):
    n_dp = len(refs) - 5
    pieces, outs, whole = refs[:n_dp], refs[n_dp:-1], refs[-1]
    n_sh, rows, width = pieces[0].shape
    for k, piece in enumerate(pieces):
        for j in range(n_sh):
            d = lax.rem(place[0] + k, n_dp)
            s = lax.rem(place[1] + j, n_sh)
            at = pl.multiple_of((d * n_sh + s) * rows, rows)
            whole[pl.ds(at, rows), :] = piece[j].astype(jnp.float32)
    at = 0
    for first, second in (outs[:2], outs[2:]):
        for c in range(0, first.shape[1], width):
            first[:, c : c + width] = whole[at : at + width, :]
            at += width
        second[...] = whole[at : at + second.shape[0], :]
        at += second.shape[0]


def spread(pieces, weights):
    place = jnp.stack([lax.axis_index("dp"), lax.axis_index("shard")]).astype(jnp.int32)
    total = sum(w.size for w in weights)
    return pl.pallas_call(
        spread_kernel,
        in_specs=[pl.BlockSpec(memory_space=pltpu.SMEM)]
        + [pl.BlockSpec(memory_space=pltpu.VMEM)] * len(pieces),
        out_specs=[pl.BlockSpec(memory_space=pltpu.VMEM)] * 4,
        out_shape=[jax.ShapeDtypeStruct(w.shape, jnp.float32) for w in weights],
        scratch_shapes=[
            pltpu.VMEM((total // pieces[0].shape[-1], pieces[0].shape[-1]), jnp.float32)
        ],
        cost_estimate=pl.CostEstimate(flops=total, transcendentals=0, bytes_accessed=6 * total),
        name="spread",
    )(place, *pieces)


def middle_kernel(n_dp, n_ex, *refs):
    expos, seen, users = refs[:n_dp], refs[n_dp : 2 * n_dp], refs[2 * n_dp : 3 * n_dp]
    own, positive, item_cot, share, loss_row = refs[3 * n_dp :]
    step = pl.program_id(0)
    totals = []
    for b in range(n_dp):
        total = seen[0][b : b + 1, :]
        for k in range(1, n_dp):
            j = (b - k) % n_dp
            total = total + seen[k][j : j + 1, :]
        totals.append(total)
    acc = jnp.zeros(item_cot.shape, jnp.float32)
    for expo, total, user in zip(expos, totals, users):
        probs = (expo[...] * (1.0 / total)).astype(jnp.bfloat16)
        acc = acc + jnp.dot(probs, user[...], preferred_element_type=jnp.float32)
    rows = item_cot.shape[0]
    own_f = own[...].astype(jnp.float32)
    acc = acc - jnp.where(step * rows < n_ex, own_f, jnp.zeros_like(own_f))
    item_cot[...] = acc / logit_divisor

    @pl.when(step == 0)
    def _():
        width = share.shape[1]
        share[...] = jnp.broadcast_to(1.0 / totals[0], (width, n_ex)).T
        pairs = users[0][...].astype(jnp.float32) * positive[...].astype(jnp.float32)
        score = jnp.sum(jnp.sum(pairs, axis=0, keepdims=True), axis=1, keepdims=True)
        loss = jnp.sum(jnp.log(totals[0]), axis=1, keepdims=True) - score / logit_divisor
        rest = jnp.broadcast_to(loss, loss_row.shape)
        lane = lax.broadcasted_iota(jnp.int32, loss_row.shape, 1)
        row = jnp.zeros(loss_row.shape, jnp.float32)
        for k in range(3):
            term = rest.astype(jnp.bfloat16).astype(jnp.float32)
            row = jnp.where(lane == k, term, row)
            rest = rest - term
        loss_row[...] = row


def middle(expos, seen, users, items):
    n_dp = len(expos)
    n_items, n_ex = expos[0].shape
    width = items.shape[1]
    rows = 256
    last = n_ex // rows - 1

    def fixed(x):
        return pl.BlockSpec(x.shape, lambda i: (0, 0))

    return pl.pallas_call(
        functools.partial(middle_kernel, n_dp, n_ex),
        grid=(n_items // rows,),
        in_specs=[pl.BlockSpec((rows, n_ex), lambda i: (i, 0))] * n_dp
        + [fixed(x) for x in seen]
        + [fixed(x) for x in users]
        + [
            pl.BlockSpec((rows, width), lambda i: (jnp.minimum(i, last), 0)),
            pl.BlockSpec((n_ex, width), lambda i: (0, 0)),
        ],
        out_specs=[
            pl.BlockSpec((rows, width), lambda i: (i, 0)),
            pl.BlockSpec((n_ex, width), lambda i: (0, 0)),
            pl.BlockSpec((1, width), lambda i: (0, 0)),
        ],
        out_shape=[
            jax.ShapeDtypeStruct((n_items, width), jnp.float32),
            jax.ShapeDtypeStruct((n_ex, width), jnp.float32),
            jax.ShapeDtypeStruct((1, width), jnp.float32),
        ],
        cost_estimate=pl.CostEstimate(
            flops=2 * n_dp * n_items * n_ex * width,
            transcendentals=n_ex,
            bytes_accessed=4 * n_dp * n_items * n_ex,
        ),
        name="middle",
    )(*expos, *seen, *users, users[0], items)


def exchange(x):
    return lax.all_to_all(x, AXES, split_axis=0, concat_axis=0, tiled=True)


def fetch(blocks, axis):
    n = lax.axis_size(axis)
    return [blocks[0]] + [
        lax.ppermute(blocks[k], axis, [((i + k) % n, i) for i in range(n)]) for k in range(1, n)
    ]


def give(blocks, axis):
    n = lax.axis_size(axis)
    return [blocks[0]] + [
        lax.ppermute(blocks[k], axis, [(i, (i + k) % n) for i in range(n)]) for k in range(1, n)
    ]


def per_device(
    id_table, ada_state, user_first, user_second, item_first, item_second, fetch_rows, lookup_slots
):
    width = id_table.shape[1]
    n_dp = lax.axis_size("dp")
    n_all = n_dp * lax.axis_size("shard")
    cap = fetch_rows.shape[-1]
    n_ex = EXAMPLES_ON_CHIP
    asked = exchange(fetch_rows.reshape(n_all, cap))
    fetched = id_table.at[asked.reshape(-1)].get(mode="promise_in_bounds")
    slot_rows = exchange(fetched.reshape(n_all, cap, width)).reshape(-1, width)
    slot_index = lookup_slots[0]
    looked = slot_rows.at[slot_index].get(mode="promise_in_bounds")

    user_vec, user_saved = tower(looked[:n_ex], user_first, user_second)
    user_bf = user_vec.astype(jnp.bfloat16)
    item_rows, user_bf = lax.optimization_barrier((looked[n_ex:], user_bf))
    group_users = fetch([user_bf] * n_dp, "dp")
    item_vec, item_saved = tower(item_rows, item_first, item_second)
    item_bf = item_vec.astype(jnp.bfloat16)

    parts, pulls, expos = [], [], []
    for block in group_users:
        expo = jnp.exp(
            jnp.dot(item_bf, block.T, preferred_element_type=jnp.float32) / logit_divisor
        )
        parts.append(jnp.sum(expo, axis=0))
        pulls.append(
            lax.dot_general(
                expo.astype(jnp.bfloat16),
                item_bf,
                (((0,), (0,)), ((), ())),
                preferred_element_type=jnp.float32,
            )
        )
        expos.append(expo)
    mine = jnp.stack(parts)
    seen = fetch([mine] * n_dp, "dp")
    returned = give([pulls[0]] + [p.astype(jnp.bfloat16) for p in pulls[1:]], "dp")
    item_cot, share, loss_row = middle(expos, seen, group_users, item_bf)
    positive = item_bf[:n_ex].astype(jnp.float32)

    item_look, item_sums = tower_back(item_saved, item_cot)
    pulled = sum(p.astype(jnp.float32) for p in returned)
    user_cot = (pulled * share - positive) / logit_divisor
    sent = exchange(
        tower_back(
            user_saved, user_cot, (item_look, item_sums, lookup_slots, loss_row), n_all, cap
        )
    )
    deep = sent.shape[1] - cap - 8
    chunk = jnp.sum(sent[:, : deep + 8].astype(jnp.float32), axis=0)
    mean_loss = jnp.sum(chunk[deep, :3]) / (n_all * n_ex)
    chunk = (chunk[:deep] / n_all).astype(jnp.bfloat16)
    row = jnp.stack(fetch([chunk] * lax.axis_size("shard"), "shard"))
    outs = spread(fetch([row] * n_dp, "dp"), (user_first, user_second, item_first, item_second))

    new_table, new_state = update(id_table, ada_state, asked.reshape(n_all, 1, cap), sent)
    return (new_table, new_state, *outs, mean_loss)


def solution(mesh):
    return jax.shard_map(
        per_device,
        mesh=mesh,
        in_specs=(
            P(("dp", "shard"), None),
            P(("dp", "shard")),
            P(),
            P(),
            P(),
            P(),
            P(("dp", "shard"), None, None, None),
            P(("dp", "shard"), None),
        ),
        out_specs=(P(("dp", "shard"), None), P(("dp", "shard")), P(), P(), P(), P(), P()),
        check_vma=False,
    )
```

```python
import functools

import jax
import jax.numpy as jnp
from jax import lax
from jax.experimental import pallas as pl
from jax.experimental.pallas import tpu as pltpu
from jax.sharding import PartitionSpec as P


EXAMPLES_ON_CHIP = 512
AXES = ("dp", "shard")

fine = lax.Precision.HIGH
logit_divisor = 0.025
learn_rate = 0.1
epsilon = 1e-08


def product(a, b, dims):
    return lax.dot_general(
        a, b, (dims, ((), ())), precision=fine, preferred_element_type=jnp.float32
    )


def tower(looked, first_w, second_w):
    hidden = product(looked, first_w, ((1,), (0,)))
    gate = jax.nn.sigmoid(hidden)
    active = hidden * gate
    out = product(active, second_w, ((1,), (0,)))
    norm = jnp.sqrt(jnp.sum(out * out, axis=1, keepdims=True) + 1e-06)
    return out / norm, (hidden, out, first_w, second_w)


def halves(x):
    high = x.astype(jnp.bfloat16)
    return high, (x - high.astype(jnp.float32)).astype(jnp.bfloat16)


def wide_dot(a, b, dims):
    def one(p, q):
        return lax.dot_general(p, q, (dims, ((), ())), preferred_element_type=jnp.float32)

    (ah, al), (bh, bl) = a, b
    return one(ah, bh) + one(al, bh) + one(ah, bl)


def back_kernel(last, *refs):
    looked, hidden, out, cot, first_w, second_w = refs[:6]
    first_g, second_g = refs[-2:]
    look_g = refs[-3] if last else refs[6]
    step = pl.program_id(0)

    @pl.when(step == 0)
    def _():
        first_g[...] = jnp.zeros_like(first_g)
        second_g[...] = jnp.zeros_like(second_g)

    z, g, h = out[...], cot[...], hidden[...]
    rows, width = z.shape
    inverse = 1.0 / jnp.sqrt(jnp.sum(z * z, axis=1, keepdims=True) + 1e-06)
    vec = z * inverse
    out_cot = (g - vec * jnp.sum(vec * g, axis=1, keepdims=True)) * inverse
    gate = 1.0 / (1.0 + jnp.exp(-h))
    active = h * gate
    slope = gate + active * (1.0 - gate)
    hidden_cot = wide_dot(halves(out_cot), halves(second_w[...]), ((1,), (1,))) * slope
    both = halves(hidden_cot)
    mine = wide_dot(both, halves(first_w[...]), ((1,), (1,))).astype(look_g.dtype)
    if last:
        look_g[pl.ds(pl.multiple_of(step * rows, rows), rows), :] = mine
    else:
        look_g[...] = mine
    first_g[...] += wide_dot(halves(looked[...].T), both, ((1,), (0,)))
    second_g[...] += wide_dot(halves(out_cot.T), halves(active), ((1,), (0,)))

    @pl.when(step == pl.num_programs(0) - 1)
    def _():
        flat = [first_g[:, c : c + width] for c in range(0, first_g.shape[1], width)]
        flat += [second_g[:, c : c + width].T for c in range(0, second_g.shape[1], width)]
        flat = [f.astype(jnp.bfloat16) for f in flat]
        if not last:
            for k, f in enumerate(flat):
                refs[7][k * width : (k + 1) * width, :] = f
            return
        item_look, item_sums, lookups, loss_row, sent = refs[6:11]
        n_all = sent.shape[0]
        deep = 2 * len(flat) * width // n_all
        cap = sent.shape[1] - deep - 8
        for k in range(n_all):
            block, at = divmod(k * deep, width)
            if block < len(flat):
                piece = flat[block][at : at + deep]
            else:
                at += (block - len(flat)) * width
                piece = item_sums[at : at + deep, :]
            sent[k, :deep, :] = piece
            sent[k, deep : deep + 8, :] = jnp.broadcast_to(loss_row[...], (8, width)).astype(
                sent.dtype
            )
        n_ex = look_g.shape[0]
        group = max(1, 576 // cap)
        user_ids, item_ids = lookups[:, :n_ex], lookups[:, n_ex:]
        for k in range(0, n_all, group):
            n = min(group, n_all - k)

            def owns(ids):
                slot = lax.broadcasted_iota(jnp.int32, (n * cap, ids.shape[1]), 0) + k * cap
                return jnp.where(slot == ids, 1.0, 0.0).astype(jnp.bfloat16)

            total = jnp.dot(owns(user_ids), look_g[...], preferred_element_type=jnp.float32)
            total += jnp.dot(owns(item_ids), item_look[...], preferred_element_type=jnp.float32)
            for j in range(n):
                sent[k + j, deep + 8 :, :] = total[j * cap : (j + 1) * cap].astype(sent.dtype)


def tower_back(looked, start, saved, cot, rest=(), n_all=0, cap=0):
    hidden, out, first_w, second_w = saved
    n, width = out.shape
    inner = hidden.shape[1]
    rows = min(n, 512)
    last = bool(rest)

    def by_rows(w):
        return pl.BlockSpec((rows, w), lambda i: (i, 0))

    def fixed(shape):
        return pl.BlockSpec(shape, lambda i: (0,) * len(shape))

    if last:
        shape = (n_all, 4 * inner // n_all + 8 + cap, width)
        out_specs = fixed(shape)
        out_shape = jax.ShapeDtypeStruct(shape, jnp.bfloat16)
        scratch = [pltpu.VMEM((n, width), jnp.bfloat16)]
    else:
        out_specs = [by_rows(width), fixed((2 * inner, width))]
        out_shape = [
            jax.ShapeDtypeStruct((n, width), jnp.bfloat16),
            jax.ShapeDtypeStruct((2 * inner, width), jnp.bfloat16),
        ]
        scratch = []
    return pl.pallas_call(
        functools.partial(back_kernel, last),
        grid=(n // rows,),
        in_specs=[pl.BlockSpec((rows, width), lambda i: (i + start // rows, 0))]
        + [by_rows(inner), by_rows(width), by_rows(width)]
        + [fixed(x.shape) for x in (first_w, second_w, *rest)],
        out_specs=out_specs,
        out_shape=out_shape,
        scratch_shapes=scratch + [pltpu.VMEM((width, inner), jnp.float32)] * 2,
        cost_estimate=pl.CostEstimate(
            flops=24 * n * width * inner,
            transcendentals=n * inner,
            bytes_accessed=4 * n * (inner + 4 * width),
        ),
        name="user_back" if last else "item_back",
    )(looked, hidden, out, cot, first_w, second_w, *rest)


def update_kernel(skip, rows_ref, grads, table, state, new_table, new_state, *totals):
    step = pl.program_id(0)

    @pl.when(step == 0)
    def _():
        for total in totals:
            total[...] = jnp.zeros_like(total)
        n_from, _, cap = rows_ref.shape
        each = n_from // len(totals)

        def body(i, carry):
            come = [grads[q * each + i, skip:, :].astype(jnp.float32) for q in range(len(totals))]
            for c in range(cap):
                for q, total in enumerate(totals):
                    row = rows_ref[q * each + i, 0, c]
                    total[pl.ds(row, 1), :] += come[q][c : c + 1, :]
            return carry

        lax.fori_loop(0, each, body, 0)

    rows, width = table.shape
    for k in range(rows // width):
        here = pl.ds(pl.multiple_of(step * rows + k * width, width), width)
        g = totals[0][here, :]
        for total in totals[1:]:
            g = g + total[here, :]
        mean = jnp.sum((g * g).T, axis=0, keepdims=True) * (1.0 / width)
        now = state[k : k + 1, :] + mean
        new_state[k : k + 1, :] = now
        scale = learn_rate / (jnp.sqrt(now) + epsilon)
        scale = jnp.broadcast_to(scale, (width, width)).T
        block = slice(k * width, (k + 1) * width)
        new_table[block, :] = table[block, :] - g * scale


def update(table, state, rows_of, grads):
    n, width = table.shape
    rows = n // 2
    lanes = 4
    state = state.reshape(-1, width)
    skip = grads.shape[1] - rows_of.shape[2]
    new_table, new_state = pl.pallas_call(
        functools.partial(update_kernel, skip),
        grid_spec=pltpu.PrefetchScalarGridSpec(
            num_scalar_prefetch=1,
            grid=(n // rows,),
            in_specs=[
                pl.BlockSpec(grads.shape, lambda i, r: (0, 0, 0)),
                pl.BlockSpec((rows, width), lambda i, r: (i, 0)),
                pl.BlockSpec((rows // width, width), lambda i, r: (i, 0)),
            ],
            out_specs=[
                pl.BlockSpec((rows, width), lambda i, r: (i, 0)),
                pl.BlockSpec((rows // width, width), lambda i, r: (i, 0)),
            ],
            scratch_shapes=[pltpu.VMEM(table.shape, jnp.float32)] * lanes,
        ),
        out_shape=[
            jax.ShapeDtypeStruct(table.shape, jnp.float32),
            jax.ShapeDtypeStruct(state.shape, jnp.float32),
        ],
        cost_estimate=pl.CostEstimate(
            flops=20 * n * width, transcendentals=n, bytes_accessed=8 * n * width
        ),
        name="update",
    )(rows_of, grads, table, state)
    return new_table, new_state.reshape(-1)


def spread_kernel(whole, *outs):
    at = 0
    for first, second in (outs[:2], outs[2:]):
        width = second.shape[1]
        for c in range(0, first.shape[1], width):
            first[:, c : c + width] = whole[at : at + width, :].astype(first.dtype)
            at += width
        second[...] = whole[at : at + second.shape[0], :].astype(second.dtype)
        at += second.shape[0]


def spread(whole, weights):
    return pl.pallas_call(
        spread_kernel,
        in_specs=[pl.BlockSpec(memory_space=pltpu.VMEM)],
        out_specs=[pl.BlockSpec(memory_space=pltpu.VMEM)] * len(weights),
        out_shape=[jax.ShapeDtypeStruct(w.shape, w.dtype) for w in weights],
        cost_estimate=pl.CostEstimate(
            flops=whole.size, transcendentals=0, bytes_accessed=6 * whole.size
        ),
        name="spread",
    )(whole)


def middle_kernel(n_dp, n_ex, *refs):
    expos, seen, users = refs[:n_dp], refs[n_dp : 2 * n_dp], refs[2 * n_dp : 3 * n_dp]
    own, positive, item_cot, share, loss_row, scaled = refs[3 * n_dp :]
    step = pl.program_id(0)
    width = share.shape[1]

    @pl.when(step == 0)
    def _():
        for b in range(n_dp):
            total = seen[0][b : b + 1, :]
            for k in range(1, n_dp):
                j = (b - k) % n_dp
                total = total + seen[k][j : j + 1, :]
            part = jnp.broadcast_to(1.0 / total, (width, n_ex)).T
            high, low = halves(users[b][...].astype(jnp.float32) * part)
            scaled[b, :, :width] = high
            scaled[b, :, width:] = low
            if b:
                continue
            share[...] = part
            pairs = users[0][...].astype(jnp.float32) * positive[...].astype(jnp.float32)
            score = jnp.sum(jnp.sum(pairs, axis=0, keepdims=True), axis=1, keepdims=True)
            loss = jnp.sum(jnp.log(total), axis=1, keepdims=True) - score / logit_divisor
            rest = jnp.broadcast_to(loss, loss_row.shape)
            lane = lax.broadcasted_iota(jnp.int32, loss_row.shape, 1)
            row = jnp.zeros(loss_row.shape, jnp.float32)
            for k in range(3):
                term = rest.astype(jnp.bfloat16).astype(jnp.float32)
                row = jnp.where(lane == k, term, row)
                rest = rest - term
            loss_row[...] = row

    acc = jnp.zeros((item_cot.shape[0], 2 * width), jnp.float32)
    for b, expo in enumerate(expos):
        acc = acc + jnp.dot(expo[...], scaled[b], preferred_element_type=jnp.float32)
    own_f = own[...].astype(jnp.float32)
    own_f = jnp.where(step * own_f.shape[0] < n_ex, own_f, jnp.zeros_like(own_f))
    item_cot[...] = (acc[:, :width] + acc[:, width:] - own_f) / logit_divisor


def middle(expos, seen, users, items):
    n_dp = len(expos)
    n_items, n_ex = expos[0].shape
    width = items.shape[1]
    rows = 256
    last = n_ex // rows - 1

    def fixed(x):
        return pl.BlockSpec(x.shape, lambda i: (0, 0))

    return pl.pallas_call(
        functools.partial(middle_kernel, n_dp, n_ex),
        grid=(n_items // rows,),
        in_specs=[pl.BlockSpec((rows, n_ex), lambda i: (i, 0))] * n_dp
        + [fixed(x) for x in seen]
        + [fixed(x) for x in users]
        + [
            pl.BlockSpec((rows, width), lambda i: (jnp.minimum(i, last), 0)),
            pl.BlockSpec((n_ex, width), lambda i: (0, 0)),
        ],
        out_specs=[
            pl.BlockSpec((rows, width), lambda i: (i, 0)),
            pl.BlockSpec((n_ex, width), lambda i: (0, 0)),
            pl.BlockSpec((1, width), lambda i: (0, 0)),
        ],
        out_shape=[
            jax.ShapeDtypeStruct((n_items, width), jnp.float32),
            jax.ShapeDtypeStruct((n_ex, width), jnp.float32),
            jax.ShapeDtypeStruct((1, width), jnp.float32),
        ],
        scratch_shapes=[pltpu.VMEM((n_dp, n_ex, 2 * width), jnp.bfloat16)],
        cost_estimate=pl.CostEstimate(
            flops=4 * n_dp * n_items * n_ex * width,
            transcendentals=n_ex,
            bytes_accessed=2 * n_dp * n_items * n_ex,
        ),
        name="middle",
    )(*expos, *seen, *users, users[0], items)


def exchange(x):
    return lax.all_to_all(x, AXES, split_axis=0, concat_axis=0, tiled=True)


def fetch(blocks, axis):
    n = lax.axis_size(axis)
    return [blocks[0]] + [
        lax.ppermute(blocks[k], axis, [((i + k) % n, i) for i in range(n)]) for k in range(1, n)
    ]


def give(blocks, axis):
    n = lax.axis_size(axis)
    return [blocks[0]] + [
        lax.ppermute(blocks[k], axis, [(i, (i + k) % n) for i in range(n)]) for k in range(1, n)
    ]


def per_device(
    id_table, ada_state, user_first, user_second, item_first, item_second, fetch_rows, lookup_slots
):
    width = id_table.shape[1]
    n_dp = lax.axis_size("dp")
    n_all = n_dp * lax.axis_size("shard")
    cap = fetch_rows.shape[-1]
    n_ex = EXAMPLES_ON_CHIP
    asked = exchange(fetch_rows.reshape(n_all, cap))
    fetched = id_table.at[asked].get(mode="promise_in_bounds")
    slot_rows = exchange(fetched).reshape(-1, width)
    slot_index = lookup_slots[0]
    looked = slot_rows.at[slot_index].get(mode="promise_in_bounds")

    user_vec, user_saved = tower(looked[:n_ex], user_first, user_second)
    user_bf = user_vec.astype(jnp.bfloat16)
    item_rows, user_bf = lax.optimization_barrier((looked[n_ex:], user_bf))
    group_users = fetch([user_bf] * n_dp, "dp")
    item_vec, item_saved = tower(item_rows, item_first, item_second)
    item_bf = item_vec.astype(jnp.bfloat16)

    parts, pulls, expos = [], [], []
    for block in group_users:
        expo = jnp.exp(
            jnp.dot(item_bf, block.T, preferred_element_type=jnp.float32) / logit_divisor
        )
        parts.append(jnp.sum(expo, axis=0))
        expos.append(expo.astype(jnp.bfloat16))
        pulls.append(
            lax.dot_general(
                expos[-1], item_bf, (((0,), (0,)), ((), ())), preferred_element_type=jnp.float32
            )
        )
    mine = jnp.stack(parts)
    seen = fetch([mine] * n_dp, "dp")
    returned = give([pulls[0]] + [p.astype(jnp.bfloat16) for p in pulls[1:]], "dp")
    item_cot, share, loss_row = middle(expos, seen, group_users, item_bf)
    positive = item_bf[:n_ex].astype(jnp.float32)

    item_look, item_sums = tower_back(looked, n_ex, item_saved, item_cot)
    pulled = sum(p.astype(jnp.float32) for p in returned)
    user_cot = (pulled * share - positive) / logit_divisor
    sent = exchange(
        tower_back(
            looked,
            0,
            user_saved,
            user_cot,
            (item_look, item_sums, lookup_slots, loss_row),
            n_all,
            cap,
        )
    )
    deep = sent.shape[1] - cap - 8
    chunk = jnp.sum(sent[:, : deep + 8].astype(jnp.float32), axis=0)
    mean_loss = jnp.sum(chunk[deep, :3]) / (n_all * n_ex)
    chunk = (chunk[:deep] / n_all).astype(jnp.bfloat16)
    whole = exchange(jnp.broadcast_to(chunk[None], (n_all, *chunk.shape))).reshape(-1, width)
    outs = spread(whole, (user_first, user_second, item_first, item_second))

    new_table, new_state = update(id_table, ada_state, asked.reshape(n_all, 1, cap), sent)
    return (new_table, new_state, *outs, mean_loss)


def solution(mesh):
    return jax.shard_map(
        per_device,
        mesh=mesh,
        in_specs=(
            P(("dp", "shard"), None),
            P(("dp", "shard")),
            P(),
            P(),
            P(),
            P(),
            P(("dp", "shard"), None, None, None),
            P(("dp", "shard"), None),
        ),
        out_specs=(P(("dp", "shard"), None), P(("dp", "shard")), P(), P(), P(), P(), P()),
        check_vma=False,
    )
```

```python
import functools

import jax
import jax.numpy as jnp
from jax import lax
from jax.experimental import pallas as pl
from jax.experimental.pallas import tpu as pltpu
from jax.sharding import PartitionSpec as P


EXAMPLES_ON_CHIP = 512
AXES = ("dp", "shard")

fine = lax.Precision.HIGH
logit_divisor = 0.025
learn_rate = 0.1
epsilon = 1e-08


def product(a, b, dims):
    return lax.dot_general(
        a, b, (dims, ((), ())), precision=fine, preferred_element_type=jnp.float32
    )


def tower(looked, first_w, second_w):
    hidden = product(looked, first_w, ((1,), (0,)))
    gate = jax.nn.sigmoid(hidden)
    active = hidden * gate
    out = product(active, second_w, ((1,), (0,)))
    norm = jnp.sqrt(jnp.sum(out * out, axis=1, keepdims=True) + 1e-06)
    return out / norm, (hidden, out, first_w, second_w)


def halves(x):
    high = x.astype(jnp.bfloat16)
    return high, (x - high.astype(jnp.float32)).astype(jnp.bfloat16)


def wide_dot(a, b, dims):
    def one(p, q):
        return lax.dot_general(p, q, (dims, ((), ())), preferred_element_type=jnp.float32)

    (ah, al), (bh, bl) = a, b
    return one(ah, bh) + one(al, bh) + one(ah, bl)


def narrow_dot(a, b, dims):
    a, b = a.astype(jnp.bfloat16), b.astype(jnp.bfloat16)
    return lax.dot_general(a, b, (dims, ((), ())), preferred_element_type=jnp.float32)


def back_kernel(last, n_cots, *refs):
    cots, refs = refs[:n_cots], refs[n_cots:]
    looked, hidden, out, first_w, second_w = refs[:5]
    first_g, second_g = refs[-2:]
    look_g = refs[-3] if last else refs[5]
    step = pl.program_id(0)

    @pl.when(step == 0)
    def _():
        first_g[...] = jnp.zeros_like(first_g)
        second_g[...] = jnp.zeros_like(second_g)

    z, h = out[...], hidden[...]
    if last:
        *pulled, share, positive = cots
        g = sum(p[...].astype(jnp.float32) for p in pulled) * share[...]
        g = (g - positive[...].astype(jnp.float32)) / logit_divisor
    else:
        g = cots[0][...]
    rows, width = z.shape
    inverse = 1.0 / jnp.sqrt(jnp.sum(z * z, axis=1, keepdims=True) + 1e-06)
    vec = z * inverse
    out_cot = (g - vec * jnp.sum(vec * g, axis=1, keepdims=True)) * inverse
    gate = 1.0 / (1.0 + jnp.exp(-h))
    active = h * gate
    slope = gate + active * (1.0 - gate)
    hidden_cot = wide_dot(halves(out_cot), halves(second_w[...]), ((1,), (1,))) * slope
    both = halves(hidden_cot)
    mine = narrow_dot(hidden_cot, first_w[...], ((1,), (1,))).astype(look_g.dtype)
    if last:
        look_g[pl.ds(pl.multiple_of(step * rows, rows), rows), :] = mine
    else:
        look_g[...] = mine
    first_g[...] += wide_dot(halves(looked[...].T), both, ((1,), (0,)))
    second_g[...] += narrow_dot(out_cot.T, active, ((1,), (0,)))

    @pl.when(step == pl.num_programs(0) - 1)
    def _():
        flat = [first_g[:, c : c + width] for c in range(0, first_g.shape[1], width)]
        flat += [second_g[:, c : c + width].T for c in range(0, second_g.shape[1], width)]
        flat = [f.astype(jnp.bfloat16) for f in flat]
        if not last:
            for k, f in enumerate(flat):
                refs[6][k * width : (k + 1) * width, :] = f
            return
        item_look, item_sums, lookups, loss_row, sent = refs[5:10]
        n_all = sent.shape[0]
        deep = 2 * len(flat) * width // n_all
        cap = sent.shape[1] - deep - 8
        for k in range(n_all):
            block, at = divmod(k * deep, width)
            if block < len(flat):
                piece = flat[block][at : at + deep]
            else:
                at += (block - len(flat)) * width
                piece = item_sums[at : at + deep, :]
            sent[k, :deep, :] = piece
            sent[k, deep : deep + 8, :] = jnp.broadcast_to(loss_row[...], (8, width)).astype(
                sent.dtype
            )
        n_ex = look_g.shape[0]
        group = max(1, 576 // cap)
        user_ids, item_ids = lookups[:, :n_ex], lookups[:, n_ex:]
        for k in range(0, n_all, group):
            n = min(group, n_all - k)

            def owns(ids):
                slot = lax.broadcasted_iota(jnp.int32, (n * cap, ids.shape[1]), 0) + k * cap
                return jnp.where(slot == ids, 1.0, 0.0).astype(jnp.bfloat16)

            total = jnp.dot(owns(user_ids), look_g[...], preferred_element_type=jnp.float32)
            total += jnp.dot(owns(item_ids), item_look[...], preferred_element_type=jnp.float32)
            for j in range(n):
                sent[k + j, deep + 8 :, :] = total[j * cap : (j + 1) * cap].astype(sent.dtype)


def tower_back(looked, start, saved, cots, rest=(), n_all=0, cap=0):
    hidden, out, first_w, second_w = saved
    n, width = out.shape
    inner = hidden.shape[1]
    rows = min(n, 512)
    last = bool(rest)

    def by_rows(w):
        return pl.BlockSpec((rows, w), lambda i: (i, 0))

    def fixed(shape):
        return pl.BlockSpec(shape, lambda i: (0,) * len(shape))

    if last:
        shape = (n_all, 4 * inner // n_all + 8 + cap, width)
        out_specs = fixed(shape)
        out_shape = jax.ShapeDtypeStruct(shape, jnp.bfloat16)
        scratch = [pltpu.VMEM((n, width), jnp.bfloat16)]
    else:
        out_specs = [by_rows(width), fixed((2 * inner, width))]
        out_shape = [
            jax.ShapeDtypeStruct((n, width), jnp.bfloat16),
            jax.ShapeDtypeStruct((2 * inner, width), jnp.bfloat16),
        ]
        scratch = []
    return pl.pallas_call(
        functools.partial(back_kernel, last, len(cots)),
        grid=(n // rows,),
        in_specs=[by_rows(width)] * len(cots)
        + [pl.BlockSpec((rows, width), lambda i: (i + start // rows, 0))]
        + [by_rows(inner), by_rows(width)]
        + [fixed(x.shape) for x in (first_w, second_w, *rest)],
        out_specs=out_specs,
        out_shape=out_shape,
        scratch_shapes=scratch + [pltpu.VMEM((width, inner), jnp.float32)] * 2,
        cost_estimate=pl.CostEstimate(
            flops=24 * n * width * inner,
            transcendentals=n * inner,
            bytes_accessed=4 * n * (inner + 4 * width),
        ),
        compiler_params=pltpu.CompilerParams(vmem_limit_bytes=32 << 20),
        name="user_back" if last else "item_back",
    )(*cots, looked, hidden, out, first_w, second_w, *rest)


def update_kernel(skip, rows_ref, grads, table, state, new_table, new_state, *totals):
    step = pl.program_id(0)

    @pl.when(step == 0)
    def _():
        for total in totals:
            total[...] = jnp.zeros_like(total)
        n_from, _, cap = rows_ref.shape
        each = n_from // len(totals)

        def body(i, carry):
            come = [grads[q * each + i, skip:, :].astype(jnp.float32) for q in range(len(totals))]
            for c in range(cap):
                for q, total in enumerate(totals):
                    row = rows_ref[q * each + i, 0, c]
                    total[pl.ds(row, 1), :] += come[q][c : c + 1, :]
            return carry

        lax.fori_loop(0, each, body, 0)

    rows, width = table.shape
    for k in range(rows // width):
        here = pl.ds(pl.multiple_of(step * rows + k * width, width), width)
        g = totals[0][here, :]
        for total in totals[1:]:
            g = g + total[here, :]
        mean = jnp.sum((g * g).T, axis=0, keepdims=True) * (1.0 / width)
        now = state[k : k + 1, :] + mean
        new_state[k : k + 1, :] = now
        scale = learn_rate / (jnp.sqrt(now) + epsilon)
        scale = jnp.broadcast_to(scale, (width, width)).T
        block = slice(k * width, (k + 1) * width)
        new_table[block, :] = table[block, :] - g * scale


def update(table, state, rows_of, grads):
    n, width = table.shape
    rows = n // 2
    lanes = 4
    state = state.reshape(-1, width)
    skip = grads.shape[1] - rows_of.shape[2]
    new_table, new_state = pl.pallas_call(
        functools.partial(update_kernel, skip),
        grid_spec=pltpu.PrefetchScalarGridSpec(
            num_scalar_prefetch=1,
            grid=(n // rows,),
            in_specs=[
                pl.BlockSpec(grads.shape, lambda i, r: (0, 0, 0)),
                pl.BlockSpec((rows, width), lambda i, r: (i, 0)),
                pl.BlockSpec((rows // width, width), lambda i, r: (i, 0)),
            ],
            out_specs=[
                pl.BlockSpec((rows, width), lambda i, r: (i, 0)),
                pl.BlockSpec((rows // width, width), lambda i, r: (i, 0)),
            ],
            scratch_shapes=[pltpu.VMEM(table.shape, jnp.float32)] * lanes,
        ),
        out_shape=[
            jax.ShapeDtypeStruct(table.shape, jnp.float32),
            jax.ShapeDtypeStruct(state.shape, jnp.float32),
        ],
        cost_estimate=pl.CostEstimate(
            flops=20 * n * width, transcendentals=n, bytes_accessed=8 * n * width
        ),
        compiler_params=pltpu.CompilerParams(vmem_limit_bytes=40 << 20),
        name="update",
    )(rows_of, grads, table, state)
    return new_table, new_state.reshape(-1)


def spread_kernel(whole, *outs):
    at = 0
    for first, second in (outs[:2], outs[2:]):
        width = second.shape[1]
        for c in range(0, first.shape[1], width):
            first[:, c : c + width] = whole[at : at + width, :].astype(first.dtype)
            at += width
        second[...] = whole[at : at + second.shape[0], :].astype(second.dtype)
        at += second.shape[0]


def spread(whole, weights):
    return pl.pallas_call(
        spread_kernel,
        in_specs=[pl.BlockSpec(memory_space=pltpu.VMEM)],
        out_specs=[pl.BlockSpec(memory_space=pltpu.VMEM)] * len(weights),
        out_shape=[jax.ShapeDtypeStruct(w.shape, w.dtype) for w in weights],
        cost_estimate=pl.CostEstimate(
            flops=whole.size, transcendentals=0, bytes_accessed=6 * whole.size
        ),
        name="spread",
    )(whole)


def middle_kernel(n_dp, n_ex, *refs):
    expos, seen, users = refs[:n_dp], refs[n_dp : 2 * n_dp], refs[2 * n_dp : 3 * n_dp]
    own, positive, item_cot, share, loss_row, scaled = refs[3 * n_dp :]
    step = pl.program_id(0)
    width = share.shape[1]

    @pl.when(step == 0)
    def _():
        for b in range(n_dp):
            total = seen[0][b : b + 1, :]
            for k in range(1, n_dp):
                j = (b - k) % n_dp
                total = total + seen[k][j : j + 1, :]
            part = jnp.broadcast_to(1.0 / total, (width, n_ex)).T
            high, low = halves(users[b][...].astype(jnp.float32) * part)
            scaled[b, :, :width] = high
            scaled[b, :, width:] = low
            if b:
                continue
            share[...] = part
            pairs = users[0][...].astype(jnp.float32) * positive[...].astype(jnp.float32)
            score = jnp.sum(jnp.sum(pairs, axis=0, keepdims=True), axis=1, keepdims=True)
            loss = jnp.sum(jnp.log(total), axis=1, keepdims=True) - score / logit_divisor
            rest = jnp.broadcast_to(loss, loss_row.shape)
            lane = lax.broadcasted_iota(jnp.int32, loss_row.shape, 1)
            row = jnp.zeros(loss_row.shape, jnp.float32)
            for k in range(3):
                term = rest.astype(jnp.bfloat16).astype(jnp.float32)
                row = jnp.where(lane == k, term, row)
                rest = rest - term
            loss_row[...] = row

    acc = jnp.zeros((item_cot.shape[0], 2 * width), jnp.float32)
    for b, expo in enumerate(expos):
        acc = acc + jnp.dot(expo[...], scaled[b], preferred_element_type=jnp.float32)
    own_f = own[...].astype(jnp.float32)
    own_f = jnp.where(step * own_f.shape[0] < n_ex, own_f, jnp.zeros_like(own_f))
    item_cot[...] = (acc[:, :width] + acc[:, width:] - own_f) / logit_divisor


def middle(expos, seen, users, items):
    n_dp = len(expos)
    n_items, n_ex = expos[0].shape
    width = items.shape[1]
    rows = 256
    last = n_ex // rows - 1

    def fixed(x):
        return pl.BlockSpec(x.shape, lambda i: (0, 0))

    return pl.pallas_call(
        functools.partial(middle_kernel, n_dp, n_ex),
        grid=(n_items // rows,),
        in_specs=[pl.BlockSpec((rows, n_ex), lambda i: (i, 0))] * n_dp
        + [fixed(x) for x in seen]
        + [fixed(x) for x in users]
        + [
            pl.BlockSpec((rows, width), lambda i: (jnp.minimum(i, last), 0)),
            pl.BlockSpec((n_ex, width), lambda i: (0, 0)),
        ],
        out_specs=[
            pl.BlockSpec((rows, width), lambda i: (i, 0)),
            pl.BlockSpec((n_ex, width), lambda i: (0, 0)),
            pl.BlockSpec((1, width), lambda i: (0, 0)),
        ],
        out_shape=[
            jax.ShapeDtypeStruct((n_items, width), jnp.float32),
            jax.ShapeDtypeStruct((n_ex, width), jnp.float32),
            jax.ShapeDtypeStruct((1, width), jnp.float32),
        ],
        scratch_shapes=[pltpu.VMEM((n_dp, n_ex, 2 * width), jnp.bfloat16)],
        cost_estimate=pl.CostEstimate(
            flops=4 * n_dp * n_items * n_ex * width,
            transcendentals=n_ex,
            bytes_accessed=2 * n_dp * n_items * n_ex,
        ),
        compiler_params=pltpu.CompilerParams(vmem_limit_bytes=32 << 20),
        name="middle",
    )(*expos, *seen, *users, users[0], items)


def exchange(x):
    return lax.all_to_all(x, AXES, split_axis=0, concat_axis=0, tiled=True)


def fetch(blocks, axis):
    n = lax.axis_size(axis)
    return [blocks[0]] + [
        lax.ppermute(blocks[k], axis, [((i + k) % n, i) for i in range(n)]) for k in range(1, n)
    ]


def give(blocks, axis):
    n = lax.axis_size(axis)
    return [blocks[0]] + [
        lax.ppermute(blocks[k], axis, [(i, (i + k) % n) for i in range(n)]) for k in range(1, n)
    ]


def per_device(
    id_table, ada_state, user_first, user_second, item_first, item_second, fetch_rows, lookup_slots
):
    width = id_table.shape[1]
    n_dp = lax.axis_size("dp")
    n_all = n_dp * lax.axis_size("shard")
    cap = fetch_rows.shape[-1]
    n_ex = EXAMPLES_ON_CHIP
    asked = exchange(fetch_rows.reshape(n_all, cap))
    fetched = id_table.at[asked].get(mode="promise_in_bounds")
    slot_rows = exchange(fetched).reshape(-1, width)
    slot_index = lookup_slots[0]
    looked = slot_rows.at[slot_index].get(mode="promise_in_bounds")

    user_vec, user_saved = tower(looked[:n_ex], user_first, user_second)
    user_bf = user_vec.astype(jnp.bfloat16)
    item_rows, user_bf = lax.optimization_barrier((looked[n_ex:], user_bf))
    group_users = fetch([user_bf] * n_dp, "dp")
    item_vec, item_saved = tower(item_rows, item_first, item_second)
    item_bf = item_vec.astype(jnp.bfloat16)

    parts, pulls, expos = [], [], []
    for block in group_users:
        expo = jnp.exp(
            jnp.dot(item_bf, block.T, preferred_element_type=jnp.float32) / logit_divisor
        )
        parts.append(jnp.sum(expo, axis=0))
        expos.append(expo.astype(jnp.bfloat16))
        pulls.append(
            lax.dot_general(
                expos[-1], item_bf, (((0,), (0,)), ((), ())), preferred_element_type=jnp.float32
            )
        )
    mine = jnp.stack(parts)
    seen = fetch([mine] * n_dp, "dp")
    returned = give([pulls[0]] + [p.astype(jnp.bfloat16) for p in pulls[1:]], "dp")
    item_cot, share, loss_row = middle(expos, seen, group_users, item_bf)

    item_look, item_sums = tower_back(looked, n_ex, item_saved, (item_cot,))
    sent = exchange(
        tower_back(
            looked,
            0,
            user_saved,
            (*returned, share, item_bf),
            (item_look, item_sums, lookup_slots, loss_row),
            n_all,
            cap,
        )
    )
    deep = sent.shape[1] - cap - 8
    chunk = jnp.sum(sent[:, : deep + 8].astype(jnp.float32), axis=0)
    mean_loss = jnp.sum(chunk[deep, :3]) / (n_all * n_ex)
    chunk = (chunk[:deep] / n_all).astype(jnp.bfloat16)
    whole = exchange(jnp.broadcast_to(chunk[None], (n_all, *chunk.shape))).reshape(-1, width)
    outs = spread(whole, (user_first, user_second, item_first, item_second))

    new_table, new_state = update(id_table, ada_state, asked.reshape(n_all, 1, cap), sent)
    return (new_table, new_state, *outs, mean_loss)


def solution(mesh):
    return jax.shard_map(
        per_device,
        mesh=mesh,
        in_specs=(
            P(("dp", "shard"), None),
            P(("dp", "shard")),
            P(),
            P(),
            P(),
            P(),
            P(("dp", "shard"), None, None, None),
            P(("dp", "shard"), None),
        ),
        out_specs=(P(("dp", "shard"), None), P(("dp", "shard")), P(), P(), P(), P(), P()),
        check_vma=False,
    )
```
